32 devices in a mesh: dp: 8 (over z, y), seq: 4 (over x, core).
Axes of the slice: x: 2, y: 2, z: 4, core: 2. Of those that a mesh axis runs over, the one named last changes fastest.
Arguments:
- tokens: bfloat16 [64, 320, 1024], P('dp', 'seq'), may hold values from -6 to 6
- keep: int32 [64, 320], P('dp'), may hold values from 0 to 1, as said below
- adapter_id: int32 [64], P('dp'), may hold values from 0 to 7
- w_qkv: bfloat16 [1024, 3072], P('dp'), may hold values from -0.1875 to 0.1875
- w_o: bfloat16 [1024, 1024], P('dp'), may hold values from -0.75 to 0.75
- w_up: bfloat16 [1024, 4096], P('dp'), may hold values from -0.1875 to 0.1875
- w_down: bfloat16 [4096, 1024], P('dp'), may hold values from -0.09375 to 0.09375
- ln1_gain: float32 [1024], replicated, may hold values from 0.1 to 1.9
- ln2_gain: float32 [1024], replicated, may hold values from 0.1 to 1.9
- qkv_in: bfloat16 [3, 8, 1024, 16], replicated, may hold values from -0.1875 to 0.1875
- qkv_out: bfloat16 [3, 8, 16, 1024], replicated, may hold values from -0.75 to 0.75
- o_in: bfloat16 [8, 1024, 16], replicated, may hold values from -0.1875 to 0.1875
- o_out: bfloat16 [8, 16, 1024], replicated, may hold values from -1.5 to 1.5
- up_in: bfloat16 [8, 1024, 16], replicated, may hold values from -0.1875 to 0.1875
- up_out: bfloat16 [8, 16, 4096], replicated, may hold values from -0.75 to 0.75
- down_in: bfloat16 [8, 4096, 16], replicated, may hold values from -0.09375 to 0.09375
- down_out: bfloat16 [8, 16, 1024], replicated, may hold values from -0.75 to 0.75
- cotangent: bfloat16 [64, 320, 1024], P('dp', 'seq'), may hold values from -6 to 6
Outputs:
- layer_out: bfloat16 [64, 320, 1024], P('dp', 'seq')
- grad_tokens: bfloat16 [64, 320, 1024], P('dp', 'seq')
- grad_qkv_in: float32 [3, 8, 1024, 16], replicated
- grad_qkv_out: float32 [3, 8, 16, 1024], replicated
- grad_o_in: float32 [8, 1024, 16], replicated
- grad_o_out: float32 [8, 16, 1024], replicated
- grad_up_in: float32 [8, 1024, 16], replicated
- grad_up_out: float32 [8, 16, 4096], replicated
- grad_down_in: float32 [8, 4096, 16], replicated
- grad_down_out: float32 [8, 16, 1024], replicated
The draws below stay inside these ranges and needn't reach their ends.
Inputs may be any that keep to these rules, and one draw needn't show every extreme that they name: `keep`: each image keeps from 40 to all 320 of its tokens, at positions spread at random.
All inputs are finite; a program needn't handle non-finite values.
Results may differ from the reference program's by a relative error of at most 0.017.
The reference program's roundings to bfloat16 on the way count: a program that leaves them out, or rounds other values in their place, can miss the bound.
Values may be sent and summed in bfloat16 or wider, within the bound.
A program may use at most 192 MiB of HBM per device.

```python
import jax
import jax.numpy as jnp
from jax import lax

D = 1024
HEADS = 16
HEAD_DIM = 64
FF = 4096
RANK = 16
ADAPT = 8
LEN = 320
IMG_DEV = 8
IMAGES = 64


def draw_keep(key, part):
    count_key = jax.random.fold_in(key, 11)
    order_key = jax.random.fold_in(key, 12)
    kept_count = jax.random.randint(count_key, (IMAGES, 1), LEN // 8, LEN + 1)
    order_score = jax.random.randint(order_key, (IMAGES, LEN), 0, 1 << 20) * LEN + jnp.arange(LEN, dtype=jnp.int32)[None, :]
    position_rank = jnp.argsort(jnp.argsort(order_score, axis=1), axis=1)
    return (position_rank < kept_count).astype(jnp.int32)


def set_ends(values, own_key, smallest, top_value):
    longest = values.shape.index(max(values.shape))
    spots = []
    for shift in (0, 1):
        where = [jax.random.randint(jax.random.fold_in(own_key, axis), (), 0, length) for axis, length in enumerate(values.shape)]
        where[longest] = (where[longest] + shift) % values.shape[longest]
        spots.append(tuple(where))
    return values.at[spots[0]].set(smallest).at[spots[1]].set(top_value)


def block_scale(rng, shape, cuts, smallest, top_value):
    level = 1.0
    for dim, shards_of in cuts:
        heights = jax.random.uniform(jax.random.fold_in(jax.random.fold_in(rng, 6), dim), (shards_of,), jnp.float32, smallest / len(cuts), top_value / len(cuts))
        level = level * jnp.repeat(jnp.exp(heights), shape[dim] // shards_of).reshape((-1,) + (1,) * (len(shape) - 1 - dim))
    return level


def scatter_about(own_key, extent, scale, most, shards=(), kind=jnp.bfloat16):
    values = jax.random.normal(own_key, extent, jnp.float32) * scale
    if len(shards) > 0:
        values = block_scale(own_key, extent, shards, -0.22, 0.18) * values
    return jnp.clip(values, min=-most, max=most).astype(kind)


def setup_inputs(seed: int = 0) -> dict:
    splits = jax.random.split(jax.random.key(seed), 19)
    return {
        "tokens": scatter_about(splits[0], (IMAGES, LEN, D), 1.0, 6.0, ((0, 8), (1, 4))),
        "keep": draw_keep(jax.random.fold_in(splits[18], 71), 0),
        "adapter_id": set_ends(jax.random.randint(splits[2], (IMAGES,), 0, ADAPT), jax.random.fold_in(splits[2], 1), 0, ADAPT - 1).astype(jnp.int32),
        "w_qkv": scatter_about(splits[3], (D, 3 * D), D ** -0.5, 0.1875, ((0, 8),)),
        "w_o": scatter_about(splits[4], (D, D), (D // 16) ** -0.5, 0.75, ((0, 8),)),
        "w_up": scatter_about(splits[5], (D, FF), D ** -0.5, 0.1875, ((0, 8),)),
        "w_down": scatter_about(splits[6], (FF, D), FF ** -0.5, 0.09375, ((0, 8),)),
        "ln1_gain": jnp.clip(1.0 + 0.18 * jax.random.normal(splits[7], (D,), jnp.float32), 0.1, 1.9),
        "ln2_gain": jnp.clip(1.0 + 0.18 * jax.random.normal(splits[8], (D,), jnp.float32), 0.1, 1.9),
        "qkv_in": scatter_about(splits[9], (3, ADAPT, D, RANK), D ** -0.5, 0.1875),
        "qkv_out": scatter_about(splits[10], (3, ADAPT, RANK, D), (4 * RANK) ** -0.5, 0.75),
        "o_in": scatter_about(splits[11], (ADAPT, D, RANK), D ** -0.5, 0.1875),
        "o_out": scatter_about(splits[12], (ADAPT, RANK, D), RANK ** -0.5, 1.5),
        "up_in": scatter_about(splits[13], (ADAPT, D, RANK), D ** -0.5, 0.1875),
        "up_out": scatter_about(splits[14], (ADAPT, RANK, FF), (4 * RANK) ** -0.5, 0.75),
        "down_in": scatter_about(splits[15], (ADAPT, FF, RANK), FF ** -0.5, 0.09375),
        "down_out": scatter_about(splits[16], (ADAPT, RANK, D), (4 * RANK) ** -0.5, 0.75),
        "cotangent": scatter_about(splits[17], (IMAGES, LEN, D), 1.0, 6.0, ((0, 8), (1, 4))),
    }


HIGHEST = lax.Precision.HIGHEST

@jax.custom_vjp
def low(v):
    return lax.optimization_barrier(v.astype(jnp.bfloat16)).astype(jnp.float32)

@jax.custom_vjp
def low_back(v):
    return v

def low_keep(v):
    return (low(v), None)

def low_pass(kept, grad):
    return (grad,)

def back_keep(v):
    return (v, None)

def back_low(kept, grad):
    return (low(grad),)
low.defvjp(low_keep, low_pass)
low_back.defvjp(back_keep, back_low)

def normalize(values, gains):
    row_mean = lax.optimization_barrier(jnp.mean(values, -1, keepdims=True))
    centred = values - row_mean
    spread = lax.optimization_barrier(jnp.mean(centred * centred, -1, keepdims=True))
    return centred * lax.rsqrt(spread + 1e-06) * gains

def adapted(inputs, weight, first_rank, second_rank):
    main = jnp.einsum('gld,de->gle', inputs, weight, precision=HIGHEST)
    reduced = low_back(low(jnp.einsum('gld,gdr->glr', inputs, first_rank, precision=HIGHEST)))
    return main + jnp.einsum('glr,gre->gle', reduced, second_rank, precision=HIGHEST)

def group_layer(frozen, adapters, tokens_f, keep_f, chosen):
    full_qkv, full_o, full_up, full_down, gain_one, gain_two = frozen
    qkv_in, qkv_out, o_in, o_out, up_in, up_out, down_in, down_out = adapters
    groups, seq_len, model_width = tokens_f.shape
    normed = low(normalize(tokens_f, gain_one))
    projected = []
    for column in range(3):
        projection = adapted(normed, full_qkv[:, column * model_width:(column + 1) * model_width], qkv_in[column][chosen], qkv_out[column][chosen])
        projected.append(low_back(low(projection)).reshape(groups, seq_len, HEADS, HEAD_DIM))
    score_scale = float(HEAD_DIM) ** (-0.5)
    scores = low_back(jnp.einsum('gqhc,gkhc->ghqk', projected[0], projected[1], precision=HIGHEST) * score_scale)
    scores = jnp.where(keep_f[:, None, None, :] > 0.5, scores, -1e+30)
    attn_probs = low(jax.nn.softmax(scores, axis=-1))
    mixed = jnp.einsum('ghqk,gkhc->gqhc', attn_probs, projected[2], precision=HIGHEST)
    mixed = low_back(low(mixed)).reshape(groups, seq_len, model_width)
    after_attn = tokens_f + low_back(adapted(mixed, full_o, o_in[chosen], o_out[chosen]))
    normed_two = low(normalize(after_attn, gain_two))
    pre_act = low_back(adapted(normed_two, full_up, up_in[chosen], up_out[chosen]))
    activated = low(jax.nn.gelu(pre_act, approximate=False))
    result = after_attn + low_back(adapted(activated, full_down, down_in[chosen], down_out[chosen]))
    return result * keep_f[:, :, None]

def reference(tokens, keep, adapter_id, w_qkv, w_o, w_up, w_down, ln1_gain, ln2_gain, qkv_in, qkv_out, o_in, o_out, up_in, up_out, down_in, down_out, cotangent):
    frozen = tuple((array.astype(jnp.float32) for array in (w_qkv, w_o, w_up, w_down, ln1_gain, ln2_gain)))
    adapters = tuple((array.astype(jnp.float32) for array in (qkv_in, qkv_out, o_in, o_out, up_in, up_out, down_in, down_out)))
    tokens_f = tokens.astype(jnp.float32)
    blocks = IMAGES // IMG_DEV
    keep_f = keep.astype(jnp.float32).reshape(blocks, IMG_DEV, LEN)
    chosen = adapter_id.astype(jnp.int32).reshape(blocks, IMG_DEV)

    def forward(inputs, params):
        stacked = inputs.reshape(blocks, IMG_DEV, LEN, D)

        def one_block(pieces):
            return jax.checkpoint(group_layer)(frozen, params, pieces[0], pieces[1], pieces[2])
        return lax.map(one_block, (stacked, keep_f, chosen)).reshape(IMAGES, LEN, D)
    output, pullback = jax.vjp(forward, tokens_f, adapters)
    grad_input, grad_adapters = pullback(cotangent.astype(jnp.float32))
    return (output.astype(jnp.bfloat16), grad_input.astype(jnp.bfloat16), grad_adapters[0], grad_adapters[1], grad_adapters[2], grad_adapters[3], grad_adapters[4], grad_adapters[5], grad_adapters[6], grad_adapters[7])
```

```python
from functools import partial

import jax
import jax.numpy as jnp
from jax import lax
from jax.experimental import pallas as pl
from jax.sharding import PartitionSpec as P

HEAD_DIM = 64
PAIR = 128


def normalize(values, gains):
    row_mean = jnp.mean(values, -1, keepdims=True)
    centred = values - row_mean
    spread = jnp.mean(centred * centred, -1, keepdims=True)
    return centred * lax.rsqrt(spread + 1e-06) * gains


def adapted(inputs, weight, first_rank, second_rank):
    main = jnp.einsum("gld,de->gle", inputs, weight, preferred_element_type=jnp.float32)
    reduced = jnp.einsum(
        "gld,gdr->glr", inputs, first_rank, preferred_element_type=jnp.float32
    ).astype(jnp.bfloat16)
    return (
        main + jnp.einsum("glr,gre->gle", reduced, second_rank, preferred_element_type=jnp.float32),
        reduced,
    )


def adapted_back(inputs, weight, first_rank, second_rank, reduced, upstream):
    grad_reduced = jnp.einsum(
        "gle,gre->glr", upstream, second_rank, preferred_element_type=jnp.float32
    ).astype(jnp.bfloat16)
    grad_second = jnp.einsum("glr,gle->gre", reduced, upstream, preferred_element_type=jnp.float32)
    grad_first = jnp.einsum(
        "gld,glr->gdr", inputs, grad_reduced, preferred_element_type=jnp.float32
    )
    grad_inputs = jnp.einsum("gle,de->gld", upstream, weight, preferred_element_type=jnp.float32)
    grad_inputs = grad_inputs + jnp.einsum(
        "glr,gdr->gld", grad_reduced, first_rank, preferred_element_type=jnp.float32
    )
    return (grad_inputs, grad_first, grad_second)


def head_masks(shape):
    lane = lax.broadcasted_iota(jnp.int32, shape, 1)
    return tuple((lane // HEAD_DIM) == half for half in range(PAIR // HEAD_DIM))


def matmul(left, right, left_dim, right_dim):
    return lax.dot_general(
        left, right, (((left_dim,), (right_dim,)), ((), ())), preferred_element_type=jnp.float32
    )


def probabilities(query, key, key_keep):
    scores = matmul(query, key, 1, 1) * (float(HEAD_DIM) ** (-0.5))
    scores = jnp.where(key_keep > 0.5, scores, -1e30)
    exponent = jnp.exp(scores - jnp.max(scores, -1, keepdims=True))
    return exponent / jnp.sum(exponent, -1, keepdims=True)


def attend_kernel(keep_ref, q_ref, k_ref, v_ref, out_ref):
    query, key, value = q_ref[0], k_ref[0], v_ref[0]
    masks = head_masks(query.shape)
    mixed = jnp.zeros(query.shape, jnp.float32)
    for mask in masks:
        probs = probabilities(jnp.where(mask, query, 0), key, keep_ref[0])
        mixed = jnp.where(mask, matmul(probs.astype(jnp.bfloat16), value, 1, 0), mixed)
    out_ref[0] = mixed.astype(jnp.bfloat16)


def attend_back_kernel(keep_ref, q_ref, k_ref, v_ref, g_ref, dq_ref, dk_ref, dv_ref):
    query, key, value, grad = q_ref[0], k_ref[0], v_ref[0], g_ref[0]
    scale = float(HEAD_DIM) ** (-0.5)
    masks = head_masks(query.shape)
    grad_q = jnp.zeros(query.shape, jnp.float32)
    grad_k, grad_v = grad_q, grad_q
    for mask in masks:
        probs = probabilities(jnp.where(mask, query, 0), key, keep_ref[0])
        grad_probs = matmul(jnp.where(mask, grad, 0), value, 1, 1)
        row_delta = jnp.sum(probs * grad_probs, -1, keepdims=True)
        grad_scores = (probs * (grad_probs - row_delta)).astype(jnp.bfloat16)
        grad_q = jnp.where(mask, matmul(grad_scores, key, 1, 0), grad_q)
        grad_k = jnp.where(mask, matmul(grad_scores, query, 0, 0), grad_k)
        grad_v = jnp.where(mask, matmul(probs.astype(jnp.bfloat16), grad, 0, 0), grad_v)
    dq_ref[0] = (grad_q * scale).astype(jnp.bfloat16)
    dk_ref[0] = (grad_k * scale).astype(jnp.bfloat16)
    dv_ref[0] = grad_v.astype(jnp.bfloat16)


def attention_call(kernel, key_keep, arrays, outputs):
    groups, seq_len, width = arrays[0].shape
    block = pl.BlockSpec((1, seq_len, PAIR), lambda g, h: (g, 0, h))
    shape = jax.ShapeDtypeStruct(arrays[0].shape, jnp.bfloat16)
    return pl.pallas_call(
        kernel,
        grid=(groups, width // PAIR),
        in_specs=[pl.BlockSpec((1, 1, seq_len), lambda g, h: (g, 0, 0))] + [block] * len(arrays),
        out_specs=[block] * outputs,
        out_shape=[shape] * outputs,
    )(key_keep[:, None, :], *arrays)


def fold_table(one_hot, per_image):
    return jnp.einsum("gi,gdr->idr", one_hot, per_image)


def gather_rows(rows):
    part = rows.shape[0] // lax.axis_size("seq")
    mine = lax.dynamic_slice_in_dim(rows, lax.axis_index("seq") * part, part, 0)
    return lax.all_gather(mine, ("dp", "seq"), axis=0, tiled=True)


def to_images(values):
    return lax.all_to_all(values, "seq", split_axis=0, concat_axis=1, tiled=True)


def to_tokens(values):
    return lax.all_to_all(values, "seq", split_axis=1, concat_axis=0, tiled=True)


def per_device(
    tokens,
    keep,
    adapter_id,
    w_qkv,
    w_o,
    w_up,
    w_down,
    ln1_gain,
    ln2_gain,
    qkv_in,
    qkv_out,
    o_in,
    o_out,
    up_in,
    up_out,
    down_in,
    down_out,
    cotangent,
):
    full_qkv = gather_rows(w_qkv)
    full_o = gather_rows(w_o)
    full_up = gather_rows(w_up)
    full_down = gather_rows(w_down)
    model_width = tokens.shape[2]
    tokens = to_images(tokens)
    cotangent = to_images(cotangent)
    groups = tokens.shape[0]
    first = lax.axis_index("seq") * groups
    keep_all = lax.dynamic_slice_in_dim(keep, first, groups, 0).astype(jnp.float32)
    adapter_id = lax.dynamic_slice_in_dim(adapter_id, first, groups, 0)
    keep_local = keep_all[:, :, None]
    sel_qkv_in = jnp.take(qkv_in, adapter_id, axis=1)
    sel_qkv_out = jnp.take(qkv_out, adapter_id, axis=1)
    sel_o_in = jnp.take(o_in, adapter_id, axis=0)
    sel_o_out = jnp.take(o_out, adapter_id, axis=0)
    sel_up_in = jnp.take(up_in, adapter_id, axis=0)
    sel_up_out = jnp.take(up_out, adapter_id, axis=0)
    sel_down_in = jnp.take(down_in, adapter_id, axis=0)
    sel_down_out = jnp.take(down_out, adapter_id, axis=0)
    tokens_f = tokens.astype(jnp.float32)
    normed = normalize(tokens_f, ln1_gain).astype(jnp.bfloat16)
    projected = []
    reduced_qkv = []
    for column in range(3):
        block_cols = full_qkv[:, column * model_width : (column + 1) * model_width]
        projection, reduced = adapted(normed, block_cols, sel_qkv_in[column], sel_qkv_out[column])
        projected.append(projection.astype(jnp.bfloat16))
        reduced_qkv.append(reduced)
    (mixed,) = attention_call(attend_kernel, keep_all, projected, 1)
    proj_o, reduced_o = adapted(mixed, full_o, sel_o_in, sel_o_out)
    after_attn = tokens_f + proj_o
    normed_two = normalize(after_attn, ln2_gain).astype(jnp.bfloat16)
    pre_act, reduced_up = adapted(normed_two, full_up, sel_up_in, sel_up_out)
    activated = jax.nn.gelu(pre_act, approximate=False).astype(jnp.bfloat16)
    proj_down, reduced_down = adapted(activated, full_down, sel_down_in, sel_down_out)
    layer_out = ((after_attn + proj_down) * keep_local).astype(jnp.bfloat16)
    one_hot = (adapter_id[:, None] == jnp.arange(qkv_in.shape[1], dtype=jnp.int32)[None, :]).astype(
        jnp.float32
    )
    grad_layer = cotangent.astype(jnp.float32) * keep_local
    grad_down = grad_layer.astype(jnp.bfloat16)
    grad_activated, down_first, down_second = adapted_back(
        activated, full_down, sel_down_in, sel_down_out, reduced_down, grad_down
    )
    gelu_value, gelu_pull = jax.vjp(partial(jax.nn.gelu, approximate=False), pre_act)
    grad_pre = gelu_pull(grad_activated)[0].astype(jnp.bfloat16)
    grad_normed_two, up_first, up_second = adapted_back(
        normed_two, full_up, sel_up_in, sel_up_out, reduced_up, grad_pre
    )
    mlp_tables = (
        fold_table(one_hot, up_first),
        fold_table(one_hot, up_second),
        fold_table(one_hot, down_first),
        fold_table(one_hot, down_second),
    )
    norm_value, norm_two_pull = jax.vjp(partial(normalize, gains=ln2_gain), after_attn)
    grad_attn = grad_layer + norm_two_pull(grad_normed_two)[0]
    grad_proj = grad_attn.astype(jnp.bfloat16)
    grad_mixed, o_first, o_second = adapted_back(
        mixed, full_o, sel_o_in, sel_o_out, reduced_o, grad_proj
    )
    out_tables = (fold_table(one_hot, o_first), fold_table(one_hot, o_second))
    early = lax.psum(mlp_tables + out_tables, ("dp", "seq"))
    grad_projected = attention_call(
        attend_back_kernel, keep_all, (*projected, grad_mixed.astype(jnp.bfloat16)), 3
    )
    grad_normed = jnp.zeros(tokens.shape, jnp.float32)
    qkv_first = []
    qkv_second = []
    for column in range(3):
        block_cols = full_qkv[:, column * model_width : (column + 1) * model_width]
        grad_part, first_part, second_part = adapted_back(
            normed,
            block_cols,
            sel_qkv_in[column],
            sel_qkv_out[column],
            reduced_qkv[column],
            grad_projected[column],
        )
        grad_normed = grad_normed + grad_part
        qkv_first.append(fold_table(one_hot, first_part))
        qkv_second.append(fold_table(one_hot, second_part))
    norm_one_value, norm_one_pull = jax.vjp(partial(normalize, gains=ln1_gain), tokens_f)
    grad_input = (grad_attn + norm_one_pull(grad_normed)[0]).astype(jnp.bfloat16)
    qkv_tables = (jnp.stack(qkv_first, 0), jnp.stack(qkv_second, 0))
    qkv_tables, early = lax.optimization_barrier((qkv_tables, early))
    late = lax.psum(qkv_tables, ("dp", "seq"))
    return (to_tokens(layer_out), to_tokens(grad_input), *late, *early[4:], *early[:4])


def solution(mesh):
    return jax.shard_map(
        per_device,
        mesh=mesh,
        in_specs=(
            P("dp", "seq", None),
            P("dp", None),
            P("dp"),
            P("dp", None),
            P("dp", None),
            P("dp", None),
            P("dp", None),
            P(),
            P(),
            P(),
            P(),
            P(),
            P(),
            P(),
            P(),
            P(),
            P(),
            P("dp", "seq", None),
        ),
        out_specs=(
            P("dp", "seq", None),
            P("dp", "seq", None),
            P(),
            P(),
            P(),
            P(),
            P(),
            P(),
            P(),
            P(),
        ),
        check_vma=False,
    )
```

```python
from functools import partial

import jax
import jax.numpy as jnp
from jax import lax
from jax.experimental import pallas as pl
from jax.experimental.pallas import tpu as pltpu
from jax.sharding import PartitionSpec as P

HEAD_DIM = 64
PAIR = 128


def normalize(values, gains):
    row_mean = jnp.mean(values, -1, keepdims=True)
    centred = values - row_mean
    spread = jnp.mean(centred * centred, -1, keepdims=True)
    return centred * lax.rsqrt(spread + 1e-06) * gains


def adapted(inputs, weight, first_rank, second_rank):
    main = jnp.einsum("gld,de->gle", inputs, weight, preferred_element_type=jnp.float32)
    reduced = jnp.einsum(
        "gld,gdr->glr", inputs, first_rank, preferred_element_type=jnp.float32
    ).astype(jnp.bfloat16)
    return (
        main + jnp.einsum("glr,gre->gle", reduced, second_rank, preferred_element_type=jnp.float32),
        reduced,
    )


def adapted_back(inputs, weight, first_rank, second_rank, reduced, upstream):
    grad_reduced = jnp.einsum(
        "gle,gre->glr", upstream, second_rank, preferred_element_type=jnp.float32
    ).astype(jnp.bfloat16)
    grad_second = jnp.einsum("glr,gle->gre", reduced, upstream, preferred_element_type=jnp.float32)
    grad_first = jnp.einsum(
        "gld,glr->grd", inputs, grad_reduced, preferred_element_type=jnp.float32
    )
    grad_inputs = jnp.einsum("gle,de->gld", upstream, weight, preferred_element_type=jnp.float32)
    grad_inputs = grad_inputs + jnp.einsum(
        "glr,gdr->gld", grad_reduced, first_rank, preferred_element_type=jnp.float32
    )
    return (grad_inputs, grad_first, grad_second)


def head_masks(shape):
    lane = lax.broadcasted_iota(jnp.int32, shape, 1)
    return tuple((lane // HEAD_DIM) == half for half in range(PAIR // HEAD_DIM))


def matmul(left, right, left_dim, right_dim):
    return lax.dot_general(
        left, right, (((left_dim,), (right_dim,)), ((), ())), preferred_element_type=jnp.float32
    )


def probabilities(query, key, key_keep):
    scores = matmul(query, key, 1, 1) * (float(HEAD_DIM) ** (-0.5))
    scores = jnp.where(key_keep > 0.5, scores, -1e30)
    exponent = jnp.exp(scores - jnp.max(scores, -1, keepdims=True))
    return exponent / jnp.sum(exponent, -1, keepdims=True)


def attend_kernel(keep_ref, q_ref, k_ref, v_ref, out_ref):
    query, key, value = q_ref[0], k_ref[0], v_ref[0]
    masks = head_masks(query.shape)
    mixed = jnp.zeros(query.shape, jnp.float32)
    for mask in masks:
        probs = probabilities(jnp.where(mask, query, 0), key, keep_ref[0])
        mixed = jnp.where(mask, matmul(probs.astype(jnp.bfloat16), value, 1, 0), mixed)
    out_ref[0] = mixed.astype(jnp.bfloat16)


def attend_back_kernel(keep_ref, q_ref, k_ref, v_ref, g_ref, dq_ref, dk_ref, dv_ref):
    query, key, value, grad = q_ref[0], k_ref[0], v_ref[0], g_ref[0]
    scale = float(HEAD_DIM) ** (-0.5)
    masks = head_masks(query.shape)
    grad_q = jnp.zeros(query.shape, jnp.float32)
    grad_k, grad_v = grad_q, grad_q
    for mask in masks:
        probs = probabilities(jnp.where(mask, query, 0), key, keep_ref[0])
        grad_probs = matmul(jnp.where(mask, grad, 0), value, 1, 1)
        row_delta = jnp.sum(probs * grad_probs, -1, keepdims=True)
        grad_scores = (probs * (grad_probs - row_delta)).astype(jnp.bfloat16)
        grad_q = jnp.where(mask, matmul(grad_scores, key, 1, 0), grad_q)
        grad_k = jnp.where(mask, matmul(grad_scores, query, 0, 0), grad_k)
        grad_v = jnp.where(mask, matmul(probs.astype(jnp.bfloat16), grad, 0, 0), grad_v)
    dq_ref[0] = (grad_q * scale).astype(jnp.bfloat16)
    dk_ref[0] = (grad_k * scale).astype(jnp.bfloat16)
    dv_ref[0] = grad_v.astype(jnp.bfloat16)


def attention_call(kernel, key_keep, arrays, outputs):
    groups, seq_len, width = arrays[0].shape
    block = pl.BlockSpec((1, seq_len, PAIR), lambda g, h: (g, 0, h))
    shape = jax.ShapeDtypeStruct(arrays[0].shape, jnp.bfloat16)
    return pl.pallas_call(
        kernel,
        grid=(groups, width // PAIR),
        in_specs=[pl.BlockSpec((1, 1, seq_len), lambda g, h: (g, 0, 0))] + [block] * len(arrays),
        out_specs=[block] * outputs,
        out_shape=[shape] * outputs,
    )(key_keep[:, None, :], *arrays)


def exchange_kernel(send_ref, full_ref, received, total, send_one, recv_one, send_two, recv_two, pass_on):
    count, groups, _, _ = send_ref.shape
    adapters, rows = total.shape[:2]
    dp, seq = lax.axis_index("dp"), lax.axis_index("seq")
    width = lax.axis_size("seq")
    me = dp * width + seq
    core = seq % 2
    sibling = me + 1 - 2 * core
    chips = count // 2

    def slice_to(target, source):
        return pltpu.make_async_remote_copy(
            send_ref.at[target],
            received.at[source],
            send_one.at[target],
            recv_one.at[source],
            device_id={"dp": target // width, "seq": target % width},
            device_id_type=pl.DeviceIdType.MESH,
        )

    def start_slice(step, carry):
        slice_to((me + step) % count, me).start()
        return carry

    lax.fori_loop(1, count, start_slice, 0)
    received[me] = send_ref[me]
    total[...] = jnp.zeros(total.shape, jnp.float32)

    def add_slice(step, carry):
        source = (me + count - step) % count

        @pl.when(step > 0)
        def _():
            slice_to(me, source).wait_recv()

        for group in range(groups):
            hot = received[source, group, :16, :].astype(jnp.float32)
            table = received[source, group, 16:, :].astype(jnp.float32)
            for adapter in range(adapters):
                total[adapter] = total[adapter] + hot[adapter : adapter + 1] * table
        return carry

    lax.fori_loop(0, count, add_slice, 0)
    full_ref[me] = total[...].astype(jnp.bfloat16)

    def block_to(target, block, sem):
        return pltpu.make_async_remote_copy(
            full_ref.at[block],
            full_ref.at[block],
            sem,
            recv_two.at[block],
            device_id={"dp": target // width, "seq": target % width},
            device_id_type=pl.DeviceIdType.MESH,
        )

    def other_chip(step):
        return ((me // 2 + step) % chips) * 2 + core

    def start_block(step, carry):
        target = other_chip(step)
        block_to(target, me, send_two.at[target // 2]).start()
        return carry

    block_to(sibling, me, pass_on.at[me // 2]).start()
    lax.fori_loop(1, chips, start_block, 0)

    def relay(step, carry):
        source = other_chip(chips - step)
        block_to(sibling, source, send_two.at[source // 2]).wait_recv()
        block_to(sibling, source, pass_on.at[source // 2]).start()
        return carry

    lax.fori_loop(1, chips, relay, 0)

    def finish(step, carry):
        source = other_chip(step)
        theirs = source + 1 - 2 * core
        block_to(sibling, theirs, pass_on.at[source // 2]).wait_recv()
        block_to(sibling, source, pass_on.at[source // 2]).wait_send()
        return carry

    lax.fori_loop(0, chips, finish, 0)

    def sent_block(step, carry):
        target = other_chip(step)
        block_to(target, me, send_two.at[target // 2]).wait_send()
        return carry

    lax.fori_loop(1, chips, sent_block, 0)

    def sent_slice(step, carry):
        slice_to((me + step) % count, me).wait_send()
        return carry

    lax.fori_loop(1, count, sent_slice, 0)


def sum_tables(tables, one_hot):
    groups, rows, columns = tables.shape
    adapters = one_hot.shape[1]
    count = lax.axis_size("dp") * lax.axis_size("seq")
    across = columns // 128
    down = count // across
    part = rows // down
    padded = -(-part // 16) * 16
    blocks = tables.astype(jnp.bfloat16).reshape(groups, down, part, across, 128)
    blocks = blocks.transpose(1, 3, 0, 2, 4).reshape(count, groups, part, 128)
    hot = jnp.pad(one_hot, ((0, 0), (0, 16 - adapters))).astype(jnp.bfloat16)
    hot = jnp.broadcast_to(hot[None, :, :, None], (count, groups, 16, 128))
    blocks = jnp.pad(blocks, ((0, 0), (0, 0), (0, padded - part), (0, 0)))
    vmem = pl.BlockSpec(memory_space=pltpu.VMEM)
    full = pl.pallas_call(
        exchange_kernel,
        in_specs=[vmem],
        out_specs=vmem,
        out_shape=jax.ShapeDtypeStruct((count, adapters, padded, 128), jnp.bfloat16),
        scratch_shapes=[
            pltpu.VMEM((count, groups, 16 + padded, 128), jnp.bfloat16),
            pltpu.VMEM((adapters, padded, 128), jnp.float32),
            pltpu.SemaphoreType.DMA((count,)),
            pltpu.SemaphoreType.DMA((count,)),
            pltpu.SemaphoreType.DMA((count // 2,)),
            pltpu.SemaphoreType.DMA((count,)),
            pltpu.SemaphoreType.DMA((count // 2,)),
        ],
        compiler_params=pltpu.CompilerParams(has_side_effects=True),
    )(jnp.concatenate([hot, blocks], 2))
    full = full[:, :, :part].reshape(down, across, adapters, part, 128)
    return full.transpose(2, 0, 3, 1, 4).reshape(adapters, rows, columns)


def gather_rows(rows):
    part = rows.shape[0] // lax.axis_size("seq")
    mine = lax.dynamic_slice_in_dim(rows, lax.axis_index("seq") * part, part, 0)
    return lax.all_gather(mine, ("dp", "seq"), axis=0, tiled=True)


def to_images(values):
    return lax.all_to_all(values, "seq", split_axis=0, concat_axis=1, tiled=True)


def to_tokens(values):
    return lax.all_to_all(values, "seq", split_axis=1, concat_axis=0, tiled=True)


def per_device(
    tokens,
    keep,
    adapter_id,
    w_qkv,
    w_o,
    w_up,
    w_down,
    ln1_gain,
    ln2_gain,
    qkv_in,
    qkv_out,
    o_in,
    o_out,
    up_in,
    up_out,
    down_in,
    down_out,
    cotangent,
):
    qkv_width = w_qkv.shape[1]
    full_qkv_o = gather_rows(jnp.concatenate([w_qkv, w_o], 1))
    full_qkv, full_o = full_qkv_o[:, :qkv_width], full_qkv_o[:, qkv_width:]
    full_up = gather_rows(w_up)
    full_down = gather_rows(w_down)
    model_width = tokens.shape[2]
    tokens = to_images(tokens)
    cotangent = to_images(cotangent)
    groups = tokens.shape[0]
    first = lax.axis_index("seq") * groups
    keep_all = lax.dynamic_slice_in_dim(keep, first, groups, 0).astype(jnp.float32)
    adapter_id = lax.dynamic_slice_in_dim(adapter_id, first, groups, 0)
    keep_local = keep_all[:, :, None]
    sel_qkv_in = jnp.take(qkv_in, adapter_id, axis=1)
    sel_qkv_out = jnp.take(qkv_out, adapter_id, axis=1)
    sel_o_in = jnp.take(o_in, adapter_id, axis=0)
    sel_o_out = jnp.take(o_out, adapter_id, axis=0)
    sel_up_in = jnp.take(up_in, adapter_id, axis=0)
    sel_up_out = jnp.take(up_out, adapter_id, axis=0)
    sel_down_in = jnp.take(down_in, adapter_id, axis=0)
    sel_down_out = jnp.take(down_out, adapter_id, axis=0)
    tokens_f = tokens.astype(jnp.float32)
    normed = normalize(tokens_f, ln1_gain).astype(jnp.bfloat16)
    projected = []
    reduced_qkv = []
    for column in range(3):
        block_cols = full_qkv[:, column * model_width : (column + 1) * model_width]
        projection, reduced = adapted(normed, block_cols, sel_qkv_in[column], sel_qkv_out[column])
        projected.append(projection.astype(jnp.bfloat16))
        reduced_qkv.append(reduced)
    (mixed,) = attention_call(attend_kernel, keep_all, projected, 1)
    proj_o, reduced_o = adapted(mixed, full_o, sel_o_in, sel_o_out)
    after_attn = tokens_f + proj_o
    normed_two = normalize(after_attn, ln2_gain).astype(jnp.bfloat16)
    pre_act, reduced_up = adapted(normed_two, full_up, sel_up_in, sel_up_out)
    activated = jax.nn.gelu(pre_act, approximate=False).astype(jnp.bfloat16)
    proj_down, reduced_down = adapted(activated, full_down, sel_down_in, sel_down_out)
    layer_out = ((after_attn + proj_down) * keep_local).astype(jnp.bfloat16)
    one_hot = (adapter_id[:, None] == jnp.arange(qkv_in.shape[1], dtype=jnp.int32)[None, :]).astype(
        jnp.float32
    )
    grad_layer = cotangent.astype(jnp.float32) * keep_local
    grad_down = grad_layer.astype(jnp.bfloat16)
    grad_activated, down_first, down_second = adapted_back(
        activated, full_down, sel_down_in, sel_down_out, reduced_down, grad_down
    )
    gelu_value, gelu_pull = jax.vjp(partial(jax.nn.gelu, approximate=False), pre_act)
    grad_pre = gelu_pull(grad_activated)[0].astype(jnp.bfloat16)
    grad_normed_two, up_first, up_second = adapted_back(
        normed_two, full_up, sel_up_in, sel_up_out, reduced_up, grad_pre
    )
    norm_value, norm_two_pull = jax.vjp(partial(normalize, gains=ln2_gain), after_attn)
    grad_attn = grad_layer + norm_two_pull(grad_normed_two)[0]
    grad_proj = grad_attn.astype(jnp.bfloat16)
    grad_mixed, o_first, o_second = adapted_back(
        mixed, full_o, sel_o_in, sel_o_out, reduced_o, grad_proj
    )
    grad_projected = attention_call(
        attend_back_kernel, keep_all, (*projected, grad_mixed.astype(jnp.bfloat16)), 3
    )
    grad_normed = jnp.zeros(tokens.shape, jnp.float32)
    qkv_first = []
    qkv_second = []
    for column in range(3):
        block_cols = full_qkv[:, column * model_width : (column + 1) * model_width]
        grad_part, first_part, second_part = adapted_back(
            normed,
            block_cols,
            sel_qkv_in[column],
            sel_qkv_out[column],
            reduced_qkv[column],
            grad_projected[column],
        )
        grad_normed = grad_normed + grad_part
        qkv_first.append(first_part)
        qkv_second.append(second_part)
    norm_one_value, norm_one_pull = jax.vjp(partial(normalize, gains=ln1_gain), tokens_f)
    grad_input = (grad_attn + norm_one_pull(grad_normed)[0]).astype(jnp.bfloat16)
    pieces = (
        *qkv_first, *qkv_second, o_first, o_second, up_first, up_second, down_first, down_second
    )
    flat = [piece.reshape(groups, -1, model_width).astype(jnp.bfloat16) for piece in pieces]
    summed = sum_tables(jnp.concatenate(flat, 1), one_hot)
    tables = []
    start = 0
    for index, (piece, rows) in enumerate(zip(pieces, flat)):
        stop = start + rows.shape[1]
        table = summed[:, start:stop].reshape(-1, *piece.shape[1:]).astype(jnp.float32)
        is_first = index < 3 or (index > 5 and index % 2 == 0)
        tables.append(table.swapaxes(1, 2) if is_first else table)
        start = stop
    return (
        to_tokens(layer_out),
        to_tokens(grad_input),
        jnp.stack(tables[:3]),
        jnp.stack(tables[3:6]),
        *tables[6:],
    )


def solution(mesh):
    return jax.shard_map(
        per_device,
        mesh=mesh,
        in_specs=(
            P("dp", "seq", None),
            P("dp", None),
            P("dp"),
            P("dp", None),
            P("dp", None),
            P("dp", None),
            P("dp", None),
            P(),
            P(),
            P(),
            P(),
            P(),
            P(),
            P(),
            P(),
            P(),
            P(),
            P("dp", "seq", None),
        ),
        out_specs=(
            P("dp", "seq", None),
            P("dp", "seq", None),
            P(),
            P(),
            P(),
            P(),
            P(),
            P(),
            P(),
            P(),
        ),
        check_vma=False,
    )
```

```python
from functools import partial

import jax
import jax.numpy as jnp
from jax import lax
from jax.experimental import pallas as pl
from jax.experimental.pallas import tpu as pltpu
from jax.sharding import PartitionSpec as P

HEAD_DIM = 64
PAIR = 128


def normalize(values, gains):
    row_mean = jnp.mean(values, -1, keepdims=True)
    centred = values - row_mean
    spread = jnp.mean(centred * centred, -1, keepdims=True)
    return centred * lax.rsqrt(spread + 1e-06) * gains


def adapted(inputs, weight, first_rank, second_rank):
    main = jnp.einsum("gld,de->gle", inputs, weight, preferred_element_type=jnp.float32)
    reduced = jnp.einsum(
        "gld,gdr->glr", inputs, first_rank, preferred_element_type=jnp.float32
    ).astype(jnp.bfloat16)
    return (
        main + jnp.einsum("glr,gre->gle", reduced, second_rank, preferred_element_type=jnp.float32),
        reduced,
    )


def adapted_back(inputs, weight, first_rank, second_rank, reduced, upstream):
    grad_reduced = jnp.einsum(
        "gle,gre->glr", upstream, second_rank, preferred_element_type=jnp.float32
    ).astype(jnp.bfloat16)
    grad_second = jnp.einsum("glr,gle->gre", reduced, upstream, preferred_element_type=jnp.float32)
    grad_first = jnp.einsum(
        "gld,glr->grd", inputs, grad_reduced, preferred_element_type=jnp.float32
    )
    grad_inputs = jnp.einsum("gle,de->gld", upstream, weight, preferred_element_type=jnp.float32)
    grad_inputs = grad_inputs + jnp.einsum(
        "glr,gdr->gld", grad_reduced, first_rank, preferred_element_type=jnp.float32
    )
    return (grad_inputs, grad_first, grad_second)


def head_masks(shape):
    lane = lax.broadcasted_iota(jnp.int32, shape, 1)
    return tuple((lane // HEAD_DIM) == half for half in range(PAIR // HEAD_DIM))


def matmul(left, right, left_dim, right_dim):
    return lax.dot_general(
        left, right, (((left_dim,), (right_dim,)), ((), ())), preferred_element_type=jnp.float32
    )


def probabilities(query, key, key_keep):
    scores = matmul(query, key, 1, 1) * (float(HEAD_DIM) ** (-0.5))
    scores = jnp.where(key_keep > 0.5, scores, -1e30)
    exponent = jnp.exp(scores - jnp.max(scores, -1, keepdims=True))
    return exponent / jnp.sum(exponent, -1, keepdims=True)


def attend_kernel(keep_ref, q_ref, k_ref, v_ref, out_ref):
    query, key, value = q_ref[0], k_ref[0], v_ref[0]
    masks = head_masks(query.shape)
    mixed = jnp.zeros(query.shape, jnp.float32)
    for mask in masks:
        probs = probabilities(jnp.where(mask, query, 0), key, keep_ref[0])
        mixed = jnp.where(mask, matmul(probs.astype(jnp.bfloat16), value, 1, 0), mixed)
    out_ref[0] = mixed.astype(jnp.bfloat16)


def attend_back_kernel(keep_ref, q_ref, k_ref, v_ref, g_ref, dq_ref, dk_ref, dv_ref):
    query, key, value, grad = q_ref[0], k_ref[0], v_ref[0], g_ref[0]
    scale = float(HEAD_DIM) ** (-0.5)
    masks = head_masks(query.shape)
    grad_q = jnp.zeros(query.shape, jnp.float32)
    grad_k, grad_v = grad_q, grad_q
    for mask in masks:
        probs = probabilities(jnp.where(mask, query, 0), key, keep_ref[0])
        grad_probs = matmul(jnp.where(mask, grad, 0), value, 1, 1)
        row_delta = jnp.sum(probs * grad_probs, -1, keepdims=True)
        grad_scores = (probs * (grad_probs - row_delta)).astype(jnp.bfloat16)
        grad_q = jnp.where(mask, matmul(grad_scores, key, 1, 0), grad_q)
        grad_k = jnp.where(mask, matmul(grad_scores, query, 0, 0), grad_k)
        grad_v = jnp.where(mask, matmul(probs.astype(jnp.bfloat16), grad, 0, 0), grad_v)
    dq_ref[0] = (grad_q * scale).astype(jnp.bfloat16)
    dk_ref[0] = (grad_k * scale).astype(jnp.bfloat16)
    dv_ref[0] = grad_v.astype(jnp.bfloat16)


def attention_call(kernel, key_keep, arrays, outputs):
    groups, seq_len, width = arrays[0].shape
    block = pl.BlockSpec((1, seq_len, PAIR), lambda g, h: (g, 0, h))
    shape = jax.ShapeDtypeStruct(arrays[0].shape, jnp.bfloat16)
    return pl.pallas_call(
        kernel,
        grid=(groups, width // PAIR),
        in_specs=[pl.BlockSpec((1, 1, seq_len), lambda g, h: (g, 0, 0))] + [block] * len(arrays),
        out_specs=[block] * outputs,
        out_shape=[shape] * outputs,
    )(key_keep[:, None, :], *arrays)


def tile_places(shapes):
    return [
        (table, row, column)
        for table, (_, rows, columns) in enumerate(shapes)
        for row in range(0, rows, 8)
        for column in range(0, columns, 128)
    ]


def exchange_kernel(stacks, shapes, hot_ref, *refs):
    tables, refs = refs[: len(shapes)], refs[len(shapes) :]
    outputs, refs = refs[: len(stacks)], refs[len(stacks) :]
    send_ref, received, total, full_ref = refs[:4]
    send_one, recv_one, recv_two, send_z, send_y, send_x, send_c = refs[4:]
    count, groups, chunk, _ = send_ref.shape
    adapters = hot_ref.shape[1]
    tiles = (chunk - adapters) // 8
    dp, seq = lax.axis_index("dp"), lax.axis_index("seq")
    width = lax.axis_size("seq")
    columns = lax.axis_size("dp") // 2
    me = dp * width + seq
    high, low = dp // 2, dp % 2
    seq_x = (seq + width // 2) % width
    seq_c = seq + 1 - 2 * (seq % 2)
    places = tile_places(shapes)

    for target in range(count):
        for group in range(groups):
            mine = places[target * tiles : (target + 1) * tiles]
            parts = [tables[t][group, r : r + 8, c : c + 128] for t, r, c in mine]
            parts += [jnp.zeros((8, 128), jnp.float32)] * (tiles - len(mine))
            parts.append(hot_ref[group])
            send_ref[target, group] = jnp.concatenate(parts, 0).astype(jnp.bfloat16)

    def remote(source_ref, target_ref, send_sem, recv_sem, target):
        return pltpu.make_async_remote_copy(
            source_ref,
            target_ref,
            send_sem,
            recv_sem,
            device_id={"dp": target // width, "seq": target % width},
            device_id_type=pl.DeviceIdType.MESH,
        )

    def slice_to(target, source):
        return remote(
            send_ref.at[target],
            received.at[source],
            send_one.at[target],
            recv_one.at[source],
            target,
        )

    def loop(start, stop, body):
        def step_body(step, carry):
            body(step)
            return carry

        lax.fori_loop(start, stop, step_body, 0)

    loop(1, count, lambda step: slice_to((me + step) % count, me).start())
    received[me] = send_ref[me]
    total[...] = jnp.zeros(total.shape, jnp.float32)

    def add_slice(step):
        source = (me + count - step) % count

        @pl.when(step > 0)
        def _():
            slice_to(me, source).wait_recv()

        for group in range(groups):
            values = received[source, group].astype(jnp.float32)
            hot = values[tiles * 8 :]
            for tile in range(tiles):
                table = values[tile * 8 : tile * 8 + 8]
                for adapter in range(adapters):
                    row = (tile * adapters + adapter) * 8
                    total[row : row + 8] = total[row : row + 8] + hot[adapter : adapter + 1] * table

    loop(0, count, add_slice)
    full_ref[me] = total[...].astype(jnp.bfloat16)

    def device(at_high, at_low, at_seq):
        return (at_high * 2 + at_low) * width + at_seq

    def block_to(target, block, sem):
        return remote(full_ref.at[block], full_ref.at[block], sem, recv_two.at[block], target)

    def along_z(step):
        return block_to(device((high + step) % columns, low, seq), me, send_z.at[step])

    def along_y(block):
        return block_to(device(high, 1 - low, seq), block, send_y.at[block])

    def along_x(block):
        return block_to(device(high, low, seq_x), block, send_x.at[block])

    def along_c(block):
        return block_to(device(high, low, seq_c), block, send_c.at[block])

    def in_column(step, at_low, at_seq):
        return device((high + columns - step) % columns, at_low, at_seq)

    loop(1, columns, lambda step: along_z(step).start())

    def from_z(step):
        block = in_column(step, low, seq)

        @pl.when(step > 0)
        def _():
            along_y(block).wait_recv()

        along_y(block).start()
        along_x(block).start()
        along_c(block).start()

    def from_y(step):
        block = in_column(step, 1 - low, seq)
        along_x(block).wait_recv()
        along_x(block).start()
        along_c(block).start()

    def from_x(at_low):
        def body(step):
            block = in_column(step, at_low, seq_x)
            along_c(block).wait_recv()
            along_c(block).start()

        return body

    def from_c(at_low, at_seq):
        return lambda step: along_c(in_column(step, at_low, at_seq)).wait_recv()

    loop(0, columns, from_z)
    loop(0, columns, from_y)
    loop(0, columns, from_x(low))
    loop(0, columns, from_x(1 - low))
    seq_xc = seq_x + 1 - 2 * (seq_x % 2)
    for at_seq in (seq_c, seq_xc):
        loop(0, columns, from_c(low, at_seq))
        loop(0, columns, from_c(1 - low, at_seq))

    for index, (table, row, column) in enumerate(places):
        block, tile = index // tiles, index % tiles
        start = tile * adapters * 8
        values = full_ref[block, start : start + adapters * 8, :].astype(jnp.float32)
        values = values.reshape(adapters, 8, 128)
        output, place = next(
            (n, table - first) for n, (first, size) in enumerate(stacks) if first <= table < first + size
        )
        outputs[output][place, :, row : row + 8, column : column + 128] = values

    loop(1, columns, lambda step: along_z(step).wait_send())
    loop(0, columns, lambda step: along_y(in_column(step, low, seq)).wait_send())
    for at_low in (low, 1 - low):
        loop(0, columns, lambda step: along_x(in_column(step, at_low, seq)).wait_send())
        for at_seq in (seq, seq_x):
            loop(0, columns, lambda step: along_c(in_column(step, at_low, at_seq)).wait_send())
    loop(1, count, lambda step: slice_to((me + step) % count, me).wait_send())


def sum_tables(tables, one_hot, stacks):
    shapes = [table.shape for table in tables]
    groups, adapters = one_hot.shape
    count = lax.axis_size("dp") * lax.axis_size("seq")
    tiles = -(-len(tile_places(shapes)) // count)
    tiles += 1 - tiles % 2
    hot = jnp.broadcast_to(one_hot[:, :, None], (groups, adapters, 128))
    vmem = pl.BlockSpec(memory_space=pltpu.VMEM)
    dma = pltpu.SemaphoreType.DMA
    return pl.pallas_call(
        partial(exchange_kernel, stacks, shapes),
        in_specs=[vmem] * (1 + len(tables)),
        out_specs=[vmem] * len(stacks),
        out_shape=[
            jax.ShapeDtypeStruct((size, adapters, *shapes[first][1:]), jnp.float32)
            for first, size in stacks
        ],
        scratch_shapes=[
            pltpu.VMEM((count, groups, tiles * 8 + adapters, 128), jnp.bfloat16),
            pltpu.VMEM((count, groups, tiles * 8 + adapters, 128), jnp.bfloat16),
            pltpu.VMEM((tiles * adapters * 8, 128), jnp.float32),
            pltpu.VMEM((count, tiles * adapters * 8, 128), jnp.bfloat16),
            dma((count,)),
            dma((count,)),
            dma((count,)),
            dma((lax.axis_size("dp") // 2,)),
            dma((count,)),
            dma((count,)),
            dma((count,)),
        ],
        compiler_params=pltpu.CompilerParams(has_side_effects=True),
    )(hot, *tables)


def gather_rows(rows):
    part = rows.shape[0] // lax.axis_size("seq")
    mine = lax.dynamic_slice_in_dim(rows, lax.axis_index("seq") * part, part, 0)
    return lax.all_gather(mine, ("dp", "seq"), axis=0, tiled=True)


def to_images(values):
    return lax.all_to_all(values, "seq", split_axis=0, concat_axis=1, tiled=True)


def to_tokens(values):
    return lax.all_to_all(values, "seq", split_axis=1, concat_axis=0, tiled=True)


def per_device(
    tokens,
    keep,
    adapter_id,
    w_qkv,
    w_o,
    w_up,
    w_down,
    ln1_gain,
    ln2_gain,
    qkv_in,
    qkv_out,
    o_in,
    o_out,
    up_in,
    up_out,
    down_in,
    down_out,
    cotangent,
):
    qkv_width = w_qkv.shape[1]
    full_qkv_o = gather_rows(jnp.concatenate([w_qkv, w_o], 1))
    full_qkv, full_o = full_qkv_o[:, :qkv_width], full_qkv_o[:, qkv_width:]
    full_up = gather_rows(w_up)
    full_down = gather_rows(w_down)
    model_width = tokens.shape[2]
    tokens = to_images(tokens)
    cotangent = to_images(cotangent)
    groups = tokens.shape[0]
    first = lax.axis_index("seq") * groups
    keep_all = lax.dynamic_slice_in_dim(keep, first, groups, 0).astype(jnp.float32)
    adapter_id = lax.dynamic_slice_in_dim(adapter_id, first, groups, 0)
    keep_local = keep_all[:, :, None]
    sel_qkv_in = jnp.take(qkv_in, adapter_id, axis=1)
    sel_qkv_out = jnp.take(qkv_out, adapter_id, axis=1)
    sel_o_in = jnp.take(o_in, adapter_id, axis=0)
    sel_o_out = jnp.take(o_out, adapter_id, axis=0)
    sel_up_in = jnp.take(up_in, adapter_id, axis=0)
    sel_up_out = jnp.take(up_out, adapter_id, axis=0)
    sel_down_in = jnp.take(down_in, adapter_id, axis=0)
    sel_down_out = jnp.take(down_out, adapter_id, axis=0)
    tokens_f = tokens.astype(jnp.float32)
    normed = normalize(tokens_f, ln1_gain).astype(jnp.bfloat16)
    projected = []
    reduced_qkv = []
    for column in range(3):
        block_cols = full_qkv[:, column * model_width : (column + 1) * model_width]
        projection, reduced = adapted(normed, block_cols, sel_qkv_in[column], sel_qkv_out[column])
        projected.append(projection.astype(jnp.bfloat16))
        reduced_qkv.append(reduced)
    (mixed,) = attention_call(attend_kernel, keep_all, projected, 1)
    proj_o, reduced_o = adapted(mixed, full_o, sel_o_in, sel_o_out)
    after_attn = tokens_f + proj_o
    normed_two = normalize(after_attn, ln2_gain).astype(jnp.bfloat16)
    pre_act, reduced_up = adapted(normed_two, full_up, sel_up_in, sel_up_out)
    activated = jax.nn.gelu(pre_act, approximate=False).astype(jnp.bfloat16)
    proj_down, reduced_down = adapted(activated, full_down, sel_down_in, sel_down_out)
    layer_out = ((after_attn + proj_down) * keep_local).astype(jnp.bfloat16)
    one_hot = (adapter_id[:, None] == jnp.arange(qkv_in.shape[1], dtype=jnp.int32)[None, :]).astype(
        jnp.float32
    )
    grad_layer = cotangent.astype(jnp.float32) * keep_local
    grad_down = grad_layer.astype(jnp.bfloat16)
    grad_activated, down_first, down_second = adapted_back(
        activated, full_down, sel_down_in, sel_down_out, reduced_down, grad_down
    )
    gelu_value, gelu_pull = jax.vjp(partial(jax.nn.gelu, approximate=False), pre_act)
    grad_pre = gelu_pull(grad_activated)[0].astype(jnp.bfloat16)
    grad_normed_two, up_first, up_second = adapted_back(
        normed_two, full_up, sel_up_in, sel_up_out, reduced_up, grad_pre
    )
    norm_value, norm_two_pull = jax.vjp(partial(normalize, gains=ln2_gain), after_attn)
    grad_attn = grad_layer + norm_two_pull(grad_normed_two)[0]
    grad_proj = grad_attn.astype(jnp.bfloat16)
    grad_mixed, o_first, o_second = adapted_back(
        mixed, full_o, sel_o_in, sel_o_out, reduced_o, grad_proj
    )
    grad_projected = attention_call(
        attend_back_kernel, keep_all, (*projected, grad_mixed.astype(jnp.bfloat16)), 3
    )
    grad_normed = jnp.zeros(tokens.shape, jnp.float32)
    qkv_first = []
    qkv_second = []
    for column in range(3):
        block_cols = full_qkv[:, column * model_width : (column + 1) * model_width]
        grad_part, first_part, second_part = adapted_back(
            normed,
            block_cols,
            sel_qkv_in[column],
            sel_qkv_out[column],
            reduced_qkv[column],
            grad_projected[column],
        )
        grad_normed = grad_normed + grad_part
        qkv_first.append(first_part)
        qkv_second.append(second_part)
    norm_one_value, norm_one_pull = jax.vjp(partial(normalize, gains=ln1_gain), tokens_f)
    grad_input = (grad_attn + norm_one_pull(grad_normed)[0]).astype(jnp.bfloat16)
    pieces = (
        *qkv_first, *qkv_second, o_first, o_second, up_first, up_second, down_first, down_second
    )
    stacks = ((0, 3), (3, 3), (6, 1), (7, 1), (8, 1), (9, 1), (10, 1), (11, 1))
    summed = sum_tables(pieces, one_hot, stacks)
    results = []
    for index, table in enumerate(summed):
        table = table if index < 2 else table[0]
        results.append(table if index % 2 else table.swapaxes(-1, -2))
    return (to_tokens(layer_out), to_tokens(grad_input), *results)


def solution(mesh):
    return jax.shard_map(
        per_device,
        mesh=mesh,
        in_specs=(
            P("dp", "seq", None),
            P("dp", None),
            P("dp"),
            P("dp", None),
            P("dp", None),
            P("dp", None),
            P("dp", None),
            P(),
            P(),
            P(),
            P(),
            P(),
            P(),
            P(),
            P(),
            P(),
            P(),
            P("dp", "seq", None),
        ),
        out_specs=(
            P("dp", "seq", None),
            P("dp", "seq", None),
            P(),
            P(),
            P(),
            P(),
            P(),
            P(),
            P(),
            P(),
        ),
        check_vma=False,
    )
```

```python
from functools import partial

import jax
import jax.numpy as jnp
from jax import lax
from jax.experimental import pallas as pl
from jax.experimental.pallas import tpu as pltpu
from jax.sharding import PartitionSpec as P

HEAD_DIM = 64
PAIR = 128


def normalize(values, gains):
    row_mean = jnp.mean(values, -1, keepdims=True)
    centred = values - row_mean
    spread = jnp.mean(centred * centred, -1, keepdims=True)
    return centred * lax.rsqrt(spread + 1e-06) * gains


def adapted(inputs, weight, first_rank, second_rank):
    main = jnp.einsum("gld,de->gle", inputs, weight, preferred_element_type=jnp.float32)
    reduced = jnp.einsum(
        "gld,gdr->glr", inputs, first_rank, preferred_element_type=jnp.float32
    ).astype(jnp.bfloat16)
    return (
        main + jnp.einsum("glr,gre->gle", reduced, second_rank, preferred_element_type=jnp.float32),
        reduced,
    )


def adapted_back(inputs, weight, first_rank, second_rank, reduced, upstream):
    grad_reduced = jnp.einsum(
        "gle,gre->glr", upstream, second_rank, preferred_element_type=jnp.float32
    ).astype(jnp.bfloat16)
    grad_second = jnp.einsum("glr,gle->gre", reduced, upstream, preferred_element_type=jnp.float32)
    grad_first = jnp.einsum(
        "gld,glr->grd", inputs, grad_reduced, preferred_element_type=jnp.float32
    )
    grad_inputs = jnp.einsum("gle,de->gld", upstream, weight, preferred_element_type=jnp.float32)
    grad_inputs = grad_inputs + jnp.einsum(
        "glr,gdr->gld", grad_reduced, first_rank, preferred_element_type=jnp.float32
    )
    return (grad_inputs, grad_first, grad_second)


def head_masks(shape):
    lane = lax.broadcasted_iota(jnp.int32, shape, 1)
    return tuple((lane // HEAD_DIM) == half for half in range(PAIR // HEAD_DIM))


def matmul(left, right, left_dim, right_dim):
    return lax.dot_general(
        left, right, (((left_dim,), (right_dim,)), ((), ())), preferred_element_type=jnp.float32
    )


def probabilities(query, key, key_keep):
    scores = matmul(query, key, 1, 1) * (float(HEAD_DIM) ** (-0.5))
    scores = jnp.where(key_keep > 0.5, scores, -1e30)
    exponent = jnp.exp(scores - jnp.max(scores, -1, keepdims=True))
    return exponent / jnp.sum(exponent, -1, keepdims=True)


def attend_kernel(keep_ref, q_ref, k_ref, v_ref, out_ref):
    query, key, value = q_ref[0], k_ref[0], v_ref[0]
    masks = head_masks(query.shape)
    mixed = jnp.zeros(query.shape, jnp.float32)
    for mask in masks:
        probs = probabilities(jnp.where(mask, query, 0), key, keep_ref[0])
        mixed = jnp.where(mask, matmul(probs.astype(jnp.bfloat16), value, 1, 0), mixed)
    out_ref[0] = mixed.astype(jnp.bfloat16)


def attend_back_kernel(keep_ref, q_ref, k_ref, v_ref, g_ref, dq_ref, dk_ref, dv_ref):
    query, key, value, grad = q_ref[0], k_ref[0], v_ref[0], g_ref[0]
    scale = float(HEAD_DIM) ** (-0.5)
    masks = head_masks(query.shape)
    grad_q = jnp.zeros(query.shape, jnp.float32)
    grad_k, grad_v = grad_q, grad_q
    for mask in masks:
        probs = probabilities(jnp.where(mask, query, 0), key, keep_ref[0])
        grad_probs = matmul(jnp.where(mask, grad, 0), value, 1, 1)
        row_delta = jnp.sum(probs * grad_probs, -1, keepdims=True)
        grad_scores = (probs * (grad_probs - row_delta)).astype(jnp.bfloat16)
        grad_q = jnp.where(mask, matmul(grad_scores, key, 1, 0), grad_q)
        grad_k = jnp.where(mask, matmul(grad_scores, query, 0, 0), grad_k)
        grad_v = jnp.where(mask, matmul(probs.astype(jnp.bfloat16), grad, 0, 0), grad_v)
    dq_ref[0] = (grad_q * scale).astype(jnp.bfloat16)
    dk_ref[0] = (grad_k * scale).astype(jnp.bfloat16)
    dv_ref[0] = grad_v.astype(jnp.bfloat16)


def attention_call(kernel, key_keep, arrays, outputs):
    groups, seq_len, width = arrays[0].shape
    block = pl.BlockSpec((1, seq_len, PAIR), lambda g, h: (g, 0, h))
    shape = jax.ShapeDtypeStruct(arrays[0].shape, jnp.bfloat16)
    return pl.pallas_call(
        kernel,
        grid=(groups, width // PAIR),
        in_specs=[pl.BlockSpec((1, 1, seq_len), lambda g, h: (g, 0, 0))] + [block] * len(arrays),
        out_specs=[block] * outputs,
        out_shape=[shape] * outputs,
    )(key_keep[:, None, :], *arrays)


def tile_places(shapes):
    return [
        (table, row, column)
        for table, (_, rows, columns) in enumerate(shapes)
        for row in range(0, rows, 8)
        for column in range(0, columns, 128)
    ]


def exchange_kernel(stacks, shapes, hot_ref, *refs):
    tables, refs = refs[: len(shapes)], refs[len(shapes) :]
    outputs, refs = refs[: len(stacks)], refs[len(stacks) :]
    send_ref, received, total, full_ref = refs[:4]
    send_one, recv_one, recv_two, send_z, send_y, send_x, send_c = refs[4:]
    count, groups, chunk, _ = send_ref.shape
    adapters = hot_ref.shape[1]
    tiles = (chunk - adapters) // 8
    dp, seq = lax.axis_index("dp"), lax.axis_index("seq")
    width = lax.axis_size("seq")
    columns = lax.axis_size("dp") // 2
    me = dp * width + seq
    high, low = dp // 2, dp % 2
    seq_x = (seq + width // 2) % width
    seq_c = seq + 1 - 2 * (seq % 2)
    places = tile_places(shapes)

    for target in range(count):
        for group in range(groups):
            mine = places[target * tiles : (target + 1) * tiles]
            parts = [tables[t][group, r : r + 8, c : c + 128] for t, r, c in mine]
            parts += [jnp.zeros((8, 128), jnp.float32)] * (tiles - len(mine))
            parts.append(hot_ref[group])
            send_ref[target, group] = jnp.concatenate(parts, 0).astype(jnp.bfloat16)

    def remote(source_ref, target_ref, send_sem, recv_sem, target):
        return pltpu.make_async_remote_copy(
            source_ref,
            target_ref,
            send_sem,
            recv_sem,
            device_id={"dp": target // width, "seq": target % width},
            device_id_type=pl.DeviceIdType.MESH,
        )

    def slice_to(target, source):
        return remote(
            send_ref.at[target],
            received.at[source],
            send_one.at[target],
            recv_one.at[source],
            target,
        )

    loop(1, count, lambda step: slice_to((me + step) % count, me).start())
    received[me] = send_ref[me]
    total[...] = jnp.zeros(total.shape, jnp.float32)

    def add_slice(step):
        source = (me + count - step) % count

        @pl.when(step > 0)
        def _():
            slice_to(me, source).wait_recv()

        for group in range(groups):
            values = received[source, group].astype(jnp.float32)
            hot = values[tiles * 8 :]
            for tile in range(tiles):
                table = values[tile * 8 : tile * 8 + 8]
                for adapter in range(adapters):
                    row = (tile * adapters + adapter) * 8
                    total[row : row + 8] = total[row : row + 8] + hot[adapter : adapter + 1] * table

    loop(0, count, add_slice)
    full_ref[me] = total[...].astype(jnp.bfloat16)

    def device(at_high, at_low, at_seq):
        return (at_high * 2 + at_low) * width + at_seq

    def block_to(target, block, sem):
        return remote(full_ref.at[block], full_ref.at[block], sem, recv_two.at[block], target)

    def along_z(step):
        return block_to(device((high + step) % columns, low, seq), me, send_z.at[step])

    def along_y(block):
        return block_to(device(high, 1 - low, seq), block, send_y.at[block])

    def along_x(block):
        return block_to(device(high, low, seq_x), block, send_x.at[block])

    def along_c(block):
        return block_to(device(high, low, seq_c), block, send_c.at[block])

    def in_column(step, at_low, at_seq):
        return device((high + columns - step) % columns, at_low, at_seq)

    loop(1, columns, lambda step: along_z(step).start())

    def from_z(step):
        block = in_column(step, low, seq)

        @pl.when(step > 0)
        def _():
            along_y(block).wait_recv()

        along_y(block).start()
        along_x(block).start()
        along_c(block).start()

    def from_y(step):
        block = in_column(step, 1 - low, seq)
        along_x(block).wait_recv()
        along_x(block).start()
        along_c(block).start()

    def from_x(at_low):
        def body(step):
            block = in_column(step, at_low, seq_x)
            along_c(block).wait_recv()
            along_c(block).start()

        return body

    def from_c(at_low, at_seq):
        return lambda step: along_c(in_column(step, at_low, at_seq)).wait_recv()

    loop(0, columns, from_z)
    loop(0, columns, from_y)
    loop(0, columns, from_x(low))
    loop(0, columns, from_x(1 - low))
    seq_xc = seq_x + 1 - 2 * (seq_x % 2)
    for at_seq in (seq_c, seq_xc):
        loop(0, columns, from_c(low, at_seq))
        loop(0, columns, from_c(1 - low, at_seq))

    for index, (table, row, column) in enumerate(places):
        block, tile = index // tiles, index % tiles
        start = tile * adapters * 8
        values = full_ref[block, start : start + adapters * 8, :].astype(jnp.float32)
        values = values.reshape(adapters, 8, 128)
        output, place = next(
            (n, table - first) for n, (first, size) in enumerate(stacks) if first <= table < first + size
        )
        outputs[output][place, :, row : row + 8, column : column + 128] = values

    loop(1, columns, lambda step: along_z(step).wait_send())
    loop(0, columns, lambda step: along_y(in_column(step, low, seq)).wait_send())
    for at_low in (low, 1 - low):
        loop(0, columns, lambda step: along_x(in_column(step, at_low, seq)).wait_send())
        for at_seq in (seq, seq_x):
            loop(0, columns, lambda step: along_c(in_column(step, at_low, at_seq)).wait_send())
    loop(1, count, lambda step: slice_to((me + step) % count, me).wait_send())


def sum_tables(tables, one_hot, stacks):
    shapes = [table.shape for table in tables]
    groups, adapters = one_hot.shape
    count = lax.axis_size("dp") * lax.axis_size("seq")
    tiles = -(-len(tile_places(shapes)) // count)
    tiles += 1 - tiles % 2
    hot = jnp.broadcast_to(one_hot[:, :, None], (groups, adapters, 128))
    vmem = pl.BlockSpec(memory_space=pltpu.VMEM)
    dma = pltpu.SemaphoreType.DMA
    return pl.pallas_call(
        partial(exchange_kernel, stacks, shapes),
        in_specs=[vmem] * (1 + len(tables)),
        out_specs=[vmem] * len(stacks),
        out_shape=[
            jax.ShapeDtypeStruct((size, adapters, *shapes[first][1:]), jnp.float32)
            for first, size in stacks
        ],
        scratch_shapes=[
            pltpu.VMEM((count, groups, tiles * 8 + adapters, 128), jnp.bfloat16),
            pltpu.VMEM((count, groups, tiles * 8 + adapters, 128), jnp.bfloat16),
            pltpu.VMEM((tiles * adapters * 8, 128), jnp.float32),
            pltpu.VMEM((count, tiles * adapters * 8, 128), jnp.bfloat16),
            dma((count,)),
            dma((count,)),
            dma((count,)),
            dma((lax.axis_size("dp") // 2,)),
            dma((count,)),
            dma((count,)),
            dma((count,)),
        ],
        compiler_params=pltpu.CompilerParams(has_side_effects=True),
    )(hot, *tables)


def loop(start, stop, body):
    def step_body(step, carry):
        body(step)
        return carry

    lax.fori_loop(start, stop, step_body, 0)


def gather_kernel(mine_ref, full_ref, arrived, send_z, send_first, send_second, send_core, local):
    dp, seq = lax.axis_index("dp"), lax.axis_index("seq")
    width = lax.axis_size("seq")
    columns = lax.axis_size("dp") // 2
    high, low = dp // 2, dp % 2
    seq_x = (seq + width // 2) % width
    seq_c = seq + 1 - 2 * (seq % 2)
    seq_xc = seq_x + 1 - 2 * (seq_x % 2)
    halves = (0, 1)

    def device(at_high, at_low, at_seq):
        return (at_high * 2 + at_low) * width + at_seq

    def remote(source_ref, target, block, half, sem):
        return pltpu.make_async_remote_copy(
            source_ref,
            full_ref.at[block, half],
            sem,
            arrived.at[block, half],
            device_id={"dp": target // width, "seq": target % width},
            device_id_type=pl.DeviceIdType.MESH,
        )

    me = device(high, low, seq)
    on_y = device(high, 1 - low, seq)
    on_x = device(high, low, seq_x)
    on_core = device(high, low, seq_c)
    first = (on_y, on_x)
    second = (on_x, on_y)

    def to_z(step, half):
        target = device((high + step) % columns, low, seq)
        return remote(mine_ref.at[half], target, me, half, send_z.at[step, half])

    def to_first(block, half):
        source = full_ref.at[block, half]
        return remote(source, first[half], block, half, send_first.at[block, half])

    def to_second(block, half):
        source = full_ref.at[block, half]
        return remote(source, second[half], block, half, send_second.at[block, half])

    def to_core(block, half):
        source = full_ref.at[block, half]
        return remote(source, on_core, block, half, send_core.at[block, half])

    def column(step, at_low, at_seq):
        return device((high + columns - step) % columns, at_low, at_seq)

    keep_mine = pltpu.make_async_copy(mine_ref, full_ref.at[me], local)
    keep_mine.start()

    def start_z(step):
        for half in halves:
            to_z(step, half).start()

    loop(1, columns, start_z)
    keep_mine.wait()

    def from_z(step):
        block = column(step, low, seq)
        for half in halves:

            @pl.when(step > 0)
            def _():
                to_core(block, half).wait_recv()

            to_first(block, half).start()
            to_second(block, half).start()
            to_core(block, half).start()

    loop(0, columns, from_z)
    by_first = ((1 - low, seq), (low, seq_x))
    by_second = (((low, seq_x), (1 - low, seq_x)), ((1 - low, seq), (1 - low, seq_x)))

    def from_first(step):
        for half in halves:
            block = column(step, *by_first[half])
            to_core(block, half).wait_recv()
            to_second(block, half).start()
            to_core(block, half).start()

    loop(0, columns, from_first)

    for place in (0, 1):

        def from_second(step):
            for half in halves:
                block = column(step, *by_second[half][place])
                to_core(block, half).wait_recv()
                to_core(block, half).start()

        loop(0, columns, from_second)

    for at_seq in (seq_c, seq_xc):
        for at_low in (low, 1 - low):

            def from_core(step):
                for half in halves:
                    to_core(column(step, at_low, at_seq), half).wait_recv()

            loop(0, columns, from_core)

    def sent_z(step):
        for half in halves:
            to_z(step, half).wait_send()

    loop(1, columns, sent_z)

    def sent_own(step):
        for half in halves:
            to_first(column(step, low, seq), half).wait_send()
            to_second(column(step, low, seq), half).wait_send()
            to_second(column(step, *by_first[half]), half).wait_send()

    loop(0, columns, sent_own)
    for at_seq in (seq, seq_x):
        for at_low in (low, 1 - low):

            def sent_core(step):
                for half in halves:
                    to_core(column(step, at_low, at_seq), half).wait_send()

            loop(0, columns, sent_core)


def gather_now(rows):
    part = rows.shape[0] // lax.axis_size("seq")
    half = rows.shape[1] // 2
    mine = lax.dynamic_slice_in_dim(rows, lax.axis_index("seq") * part, part, 0)
    mine = jnp.stack([mine[:, :half], mine[:, half:]])
    count = lax.axis_size("dp") * lax.axis_size("seq")
    vmem = pl.BlockSpec(memory_space=pltpu.VMEM)
    dma = pltpu.SemaphoreType.DMA
    full = pl.pallas_call(
        gather_kernel,
        in_specs=[vmem],
        out_specs=vmem,
        out_shape=jax.ShapeDtypeStruct((count, *mine.shape), mine.dtype),
        scratch_shapes=[
            dma((count, 2)),
            dma((lax.axis_size("dp") // 2, 2)),
            dma((count, 2)),
            dma((count, 2)),
            dma((count, 2)),
            dma,
        ],
        compiler_params=pltpu.CompilerParams(has_side_effects=True),
    )(mine)
    return full


def gather_rows(rows):
    part = rows.shape[0] // lax.axis_size("seq")
    mine = lax.dynamic_slice_in_dim(rows, lax.axis_index("seq") * part, part, 0)
    return lax.all_gather(mine, ("dp", "seq"), axis=0, tiled=True)


def to_images(values):
    return lax.all_to_all(values, "seq", split_axis=0, concat_axis=1, tiled=True)


def to_tokens(values):
    return lax.all_to_all(values, "seq", split_axis=1, concat_axis=0, tiled=True)


def per_device(
    tokens,
    keep,
    adapter_id,
    w_qkv,
    w_o,
    w_up,
    w_down,
    ln1_gain,
    ln2_gain,
    qkv_in,
    qkv_out,
    o_in,
    o_out,
    up_in,
    up_out,
    down_in,
    down_out,
    cotangent,
):
    gathered = gather_now(jnp.concatenate([w_qkv, w_o], 1))
    quarters = jnp.split(gathered.reshape(-1, 2, gathered.shape[2], 2, w_o.shape[1]), 2, 3)
    quarters = [
        quarters[place][:, half, :, 0].reshape(-1, w_o.shape[1])
        for half in (0, 1)
        for place in (0, 1)
    ]
    full_o = quarters[3]
    full_up = gather_rows(w_up)
    full_down = gather_rows(w_down)
    model_width = tokens.shape[2]
    tokens = to_images(tokens)
    cotangent = to_images(cotangent)
    groups = tokens.shape[0]
    first = lax.axis_index("seq") * groups
    keep_all = lax.dynamic_slice_in_dim(keep, first, groups, 0).astype(jnp.float32)
    adapter_id = lax.dynamic_slice_in_dim(adapter_id, first, groups, 0)
    keep_local = keep_all[:, :, None]
    sel_qkv_in = jnp.take(qkv_in, adapter_id, axis=1)
    sel_qkv_out = jnp.take(qkv_out, adapter_id, axis=1)
    sel_o_in = jnp.take(o_in, adapter_id, axis=0)
    sel_o_out = jnp.take(o_out, adapter_id, axis=0)
    sel_up_in = jnp.take(up_in, adapter_id, axis=0)
    sel_up_out = jnp.take(up_out, adapter_id, axis=0)
    sel_down_in = jnp.take(down_in, adapter_id, axis=0)
    sel_down_out = jnp.take(down_out, adapter_id, axis=0)
    tokens_f = tokens.astype(jnp.float32)
    normed = normalize(tokens_f, ln1_gain).astype(jnp.bfloat16)
    projected = []
    reduced_qkv = []
    for column in range(3):
        block_cols = quarters[column]
        projection, reduced = adapted(normed, block_cols, sel_qkv_in[column], sel_qkv_out[column])
        projected.append(projection.astype(jnp.bfloat16))
        reduced_qkv.append(reduced)
    (mixed,) = attention_call(attend_kernel, keep_all, projected, 1)
    proj_o, reduced_o = adapted(mixed, full_o, sel_o_in, sel_o_out)
    after_attn = tokens_f + proj_o
    normed_two = normalize(after_attn, ln2_gain).astype(jnp.bfloat16)
    pre_act, reduced_up = adapted(normed_two, full_up, sel_up_in, sel_up_out)
    activated = jax.nn.gelu(pre_act, approximate=False).astype(jnp.bfloat16)
    proj_down, reduced_down = adapted(activated, full_down, sel_down_in, sel_down_out)
    layer_out = ((after_attn + proj_down) * keep_local).astype(jnp.bfloat16)
    one_hot = (adapter_id[:, None] == jnp.arange(qkv_in.shape[1], dtype=jnp.int32)[None, :]).astype(
        jnp.float32
    )
    grad_layer = cotangent.astype(jnp.float32) * keep_local
    grad_down = grad_layer.astype(jnp.bfloat16)
    grad_activated, down_first, down_second = adapted_back(
        activated, full_down, sel_down_in, sel_down_out, reduced_down, grad_down
    )
    gelu_value, gelu_pull = jax.vjp(partial(jax.nn.gelu, approximate=False), pre_act)
    grad_pre = gelu_pull(grad_activated)[0].astype(jnp.bfloat16)
    grad_normed_two, up_first, up_second = adapted_back(
        normed_two, full_up, sel_up_in, sel_up_out, reduced_up, grad_pre
    )
    norm_value, norm_two_pull = jax.vjp(partial(normalize, gains=ln2_gain), after_attn)
    grad_attn = grad_layer + norm_two_pull(grad_normed_two)[0]
    grad_proj = grad_attn.astype(jnp.bfloat16)
    grad_mixed, o_first, o_second = adapted_back(
        mixed, full_o, sel_o_in, sel_o_out, reduced_o, grad_proj
    )
    grad_projected = attention_call(
        attend_back_kernel, keep_all, (*projected, grad_mixed.astype(jnp.bfloat16)), 3
    )
    grad_normed = jnp.zeros(tokens.shape, jnp.float32)
    qkv_first = []
    qkv_second = []
    for column in range(3):
        block_cols = quarters[column]
        grad_part, first_part, second_part = adapted_back(
            normed,
            block_cols,
            sel_qkv_in[column],
            sel_qkv_out[column],
            reduced_qkv[column],
            grad_projected[column],
        )
        grad_normed = grad_normed + grad_part
        qkv_first.append(first_part)
        qkv_second.append(second_part)
    norm_one_value, norm_one_pull = jax.vjp(partial(normalize, gains=ln1_gain), tokens_f)
    grad_input = (grad_attn + norm_one_pull(grad_normed)[0]).astype(jnp.bfloat16)
    pieces = (
        *qkv_first, *qkv_second, o_first, o_second, up_first, up_second, down_first, down_second
    )
    stacks = ((0, 3), (3, 3), (6, 1), (7, 1), (8, 1), (9, 1), (10, 1), (11, 1))
    summed = sum_tables(pieces, one_hot, stacks)
    results = []
    for index, table in enumerate(summed):
        table = table if index < 2 else table[0]
        results.append(table if index % 2 else table.swapaxes(-1, -2))
    return (to_tokens(layer_out), to_tokens(grad_input), *results)


def solution(mesh):
    return jax.shard_map(
        per_device,
        mesh=mesh,
        in_specs=(
            P("dp", "seq", None),
            P("dp", None),
            P("dp"),
            P("dp", None),
            P("dp", None),
            P("dp", None),
            P("dp", None),
            P(),
            P(),
            P(),
            P(),
            P(),
            P(),
            P(),
            P(),
            P(),
            P(),
            P("dp", "seq", None),
        ),
        out_specs=(
            P("dp", "seq", None),
            P("dp", "seq", None),
            P(),
            P(),
            P(),
            P(),
            P(),
            P(),
            P(),
            P(),
        ),
        check_vma=False,
    )
```
